32 devices in a mesh: freq: 4 (over y, core), tile: 8 (over z, x).
Axes of the slice: x: 2, y: 2, z: 4, core: 2. Of those that a mesh axis runs over, the one named last changes fastest.
Arguments:
- wavefield: bfloat16 [4, 3072, 256], P('freq', 'tile'), may hold values from -6 to 6
- column_bases: bfloat16 [4, 8, 8, 384, 256], P('freq', 'tile'), may hold values from -0.3125 to 0.3125
- row_bases: bfloat16 [4, 8, 8, 384, 256], P('freq', 'tile'), may hold values from -0.1875 to 0.1875
- tile_ranks: int32 [8, 8], replicated, may hold values from 16 to 128, as said below
- row_order: int32 [8], replicated, may hold values from 0 to 7, each once
- shrink_level: float32 [128], P('freq'), may hold values from 0.5 to 3
Outputs:
- shrunk: float32 [12, 128, 3072], P(None, 'freq', 'tile')
The draws below stay inside these ranges and needn't reach their ends.
Inputs may be any that keep to these rules, and one draw needn't show every extreme that they name: `tile_ranks`: each tile's rank lies between 16 and 128; both ends occur in every draw. `row_order`: A permutation of the 8 tile rows.
All inputs are finite; a program needn't handle non-finite values.
Results may differ from the reference program's by a relative error of at most 0.0044.
Values may be sent and summed in bfloat16 or wider, within the bound.
A program may use at most 64 MiB of HBM per device.

```python
import math
import jax
import jax.numpy as jnp
from jax import lax

TILE = 384
RANK = 128
NV = 128
NF = 4
NT = 12
NTR = 8
NTC = 8
NC = 3072


def draw_tile_ranks(key, part):
    key_main = jax.random.fold_in(key, 17)
    key_cap, key_base, key_top, key_bottom = jax.random.split(key_main, 4)
    rank_floor = RANK // 8
    low_column = jax.random.randint(key_cap, (NTC,), 0, 8) == 0
    rank_cap = jnp.where(low_column, RANK // 2, RANK)
    spread_width = rank_cap // 8
    base_bits = jax.random.randint(key_base, (NTR, NTC), 0, 1 << 20)
    drawn = rank_cap[None, :] - base_bits % (spread_width[None, :] + 1)
    total_tiles = NTR * NTC
    top_place = jax.random.randint(key_top, (), 0, total_tiles)
    bottom_place = (top_place + 1 + jax.random.randint(key_bottom, (), 0, total_tiles - 1)) % total_tiles
    flat_ranks = drawn.reshape(total_tiles).at[top_place].set(RANK).at[bottom_place].set(rank_floor)
    return flat_ranks.reshape(NTR, NTC).astype(jnp.int32)


def levels(stream_key, shape, shards, smallest, largest):
    def one(position, parts):
        steps = jax.random.uniform(jax.random.fold_in(jax.random.fold_in(stream_key, 6), position), (parts,), jnp.float32, smallest / len(shards), largest / len(shards))
        return jnp.repeat(jnp.exp(steps), shape[position] // parts).reshape((-1,) + (1,) * (len(shape) - position - 1))

    loudness = one(*shards[0])
    for cut in shards[1:]:
        loudness = loudness * one(*cut)
    return loudness


def centred(stream_key, dims, spread, bound, cuts=(), held_as=jnp.bfloat16):
    factor_of = levels(stream_key, dims, cuts, -0.22, 0.18) if cuts else 1.0
    result = jax.random.normal(stream_key, dims, jnp.float32) * spread * factor_of
    return jnp.minimum(jnp.maximum(result, -bound), bound).astype(held_as)


def setup_inputs(seed: int = 0) -> dict:
    streams_of = jax.random.split(jax.random.key(seed), 7)
    wavefield = centred(streams_of[0], (NF, NC, 2 * NV), 1.0, 6.0, ((0, 4), (1, 8)))
    column_bases = centred(streams_of[1], (NF, NTC, NTR, TILE, 2 * RANK), TILE ** -0.5, 0.3125, ((0, 4), (1, 8)))
    row_bases = centred(streams_of[2], (NF, NTR, NTC, TILE, 2 * RANK), (RANK * NTC) ** -0.5, 0.1875, ((0, 4), (1, 8)))
    tile_ranks = draw_tile_ranks(jax.random.fold_in(streams_of[6], 71), 0)
    row_order = jax.random.permutation(streams_of[4], NTR).astype(jnp.int32)
    shrink_level = jnp.clip(jnp.exp(math.log(3.0) - 1.7917595 * jax.random.uniform(streams_of[5], (NV,), jnp.float32) ** levels(streams_of[5], (NV,), ((0, 4),), -0.2, 0.2)), 0.5, 3.0)
    return dict(wavefield=wavefield, column_bases=column_bases, row_bases=row_bases, tile_ranks=tile_ranks, row_order=row_order, shrink_level=shrink_level)


def reference(wavefield, column_bases, row_bases, tile_ranks, row_order, shrink_level):
    keep_mask = (jnp.arange(RANK, dtype=jnp.int32)[None, None, :] < jnp.transpose(tile_ranks)[:, :, None]).astype(jnp.float32)

    def per_frequency(inputs):
        wave_now, v_now, u_now = inputs
        wave_tiles = wave_now.reshape(NTC, TILE, 2 * NV).astype(jnp.float32)
        products = jnp.einsum('jitk,jtv->jikv', v_now.astype(jnp.float32), wave_tiles)
        real_part = products[:, :, :RANK, :NV] + products[:, :, RANK:, NV:]
        imag_part = products[:, :, :RANK, NV:] - products[:, :, RANK:, :NV]
        blocks = jnp.concatenate([real_part, imag_part], axis=3) * keep_mask[:, :, :, None]
        blocks = blocks.astype(jnp.bfloat16)
        slotted = jnp.take(blocks, row_order, axis=1)
        rotated = jnp.concatenate([-slotted[:, :, :, NV:], slotted[:, :, :, :NV]], axis=3)
        stacked = jnp.concatenate([slotted, rotated], axis=2).reshape(NTC, NTR, 2 * RANK, 2, NV)
        spectrum = jnp.einsum('sjtk,jskcv->cvst', u_now.astype(jnp.float32), stacked.astype(jnp.float32))
        return spectrum.reshape(2, NV, NTR * TILE).astype(jnp.bfloat16)
    spectrum = lax.map(per_frequency, (wavefield, column_bases, row_bases))
    freq_ids = jnp.arange(NF, dtype=jnp.int32) + 1
    time_ids = jnp.arange(NT, dtype=jnp.int32)
    phase = freq_ids[:, None] * time_ids[None, :] % NT
    angle = phase.astype(jnp.float32) * (2.0 * math.pi / NT)
    cosine = jnp.cos(angle) / math.sqrt(NF)
    sine_table = jnp.sin(angle) / math.sqrt(NF)
    values = spectrum.astype(jnp.float32)
    signal = jnp.einsum('ft,fvn->tvn', cosine, values[:, 0], precision=lax.Precision.HIGHEST) - jnp.einsum('ft,fvn->tvn', sine_table, values[:, 1], precision=lax.Precision.HIGHEST)
    return signal ** 3 / (signal ** 2 + shrink_level[None, :, None] ** 2)
```

```python
import functools
import math

import jax
import jax.numpy as jnp
from jax import lax
from jax.experimental import pallas as pl
from jax.experimental.pallas import tpu as pltpu
from jax.sharding import PartitionSpec as P

MESH = pl.DeviceIdType.MESH


def target(tile, k, n):
    half = n // 2
    late = tile // half
    place = tile * late + (n - 1 - tile) * (1 - late)
    end = place // (n - n // 4)
    turn = (k + half * end) % (n - 1)
    other = turn + (turn + n - place) // n
    return other * late + (n - 1 - other) * (1 - late)


def exchange_kernel(n, nf, gs, wave, v_hbm, u_hbm, ranks_hbm, order_hbm,
                    spec_out,
                    x_buf, v_buf, u_buf, ranks, order, sending, landing,
                    spec_sending, spec_landing,
                    load_sems, v_sems, send_sems, recv_sems, spec_send_sems, spec_recv_sems):
    tile = lax.axis_index("tile")
    freq = lax.axis_index("freq")
    tile_rows = x_buf.shape[0]
    sources = x_buf.shape[1] // 2
    width = v_buf.shape[2] // 2
    chunk = sources // nf
    ng = nf // gs
    rows = gs * chunk
    targets = [target(tile, k, n) for k in range(n - 1)]

    loads = [
        pltpu.make_async_copy(wave.at[0], x_buf, load_sems.at[0]),
        pltpu.make_async_copy(ranks_hbm, ranks, load_sems.at[2]),
        pltpu.make_async_copy(order_hbm, order, load_sems.at[3]),
    ]
    v_loads = [pltpu.make_async_copy(v_hbm.at[0, 0, i], v_buf.at[i], v_sems.at[i]) for i in range(n)]
    u_load = pltpu.make_async_copy(u_hbm.at[0, 0], u_buf, load_sems.at[1])
    for load in loads + v_loads:
        load.start()

    barrier = pltpu.get_barrier_semaphore()
    for other in targets:
        pl.semaphore_signal(barrier, inc=1, device_id={"tile": other}, device_id_type=MESH)
    for hop in range(1, nf):
        pl.semaphore_signal(
            barrier, inc=1, device_id={"freq": (freq + hop) % nf}, device_id_type=MESH
        )

    def group_of(p):
        return (freq // gs + 1 + p) % ng

    def send(p, k):
        return pltpu.make_async_remote_copy(
            src_ref=sending.at[k, group_of(p)],
            dst_ref=landing.at[p, tile],
            send_sem=send_sems.at[p, k],
            recv_sem=recv_sems.at[p, tile],
            device_id={"tile": targets[k]},
            device_id_type=MESH,
        )

    def arrival(p, k):
        return pltpu.make_async_remote_copy(
            src_ref=sending.at[k, group_of(p)],
            dst_ref=landing.at[p, targets[k]],
            send_sem=send_sems.at[p, k],
            recv_sem=recv_sems.at[p, targets[k]],
            device_id={"tile": targets[k]},
            device_id_type=MESH,
        )

    def receiver_of(q):
        p, c = q // gs, q % gs
        return group_of(p) * gs + (freq + 1 + c) % gs

    def spec_send(q):
        return pltpu.make_async_remote_copy(
            src_ref=spec_sending.at[q],
            dst_ref=spec_landing.at[freq],
            send_sem=spec_send_sems.at[q],
            recv_sem=spec_recv_sems.at[freq],
            device_id={"freq": receiver_of(q)},
            device_id_type=MESH,
        )

    def spec_arrival(q, source):
        return pltpu.make_async_remote_copy(
            src_ref=spec_sending.at[q],
            dst_ref=spec_landing.at[source],
            send_sem=spec_send_sems.at[q],
            recv_sem=spec_recv_sems.at[source],
            device_id={"freq": receiver_of(q)},
            device_id_type=MESH,
        )

    for load in loads:
        load.wait()
    x_t = x_buf[...].T
    for load in v_loads:
        load.wait()
    u_load.start()

    lane = lax.broadcasted_iota(jnp.int32, (sources, width), 1)

    def make_block(k, slot):
        row = order[slot]
        rank = ranks[row, tile]
        product = jnp.dot(x_t, v_buf[row], preferred_element_type=jnp.float32)
        keep = lane < rank
        real = product[:sources, :width] + product[sources:, width:]
        imag = product[sources:, :width] - product[:sources, width:]
        real = jnp.where(keep, real, 0.0).astype(jnp.bfloat16)
        imag = jnp.where(keep, imag, 0.0).astype(jnp.bfloat16)
        for g in range(ng):
            sending[k, g, 0] = real[g * rows:(g + 1) * rows]
            sending[k, g, 1] = imag[g * rows:(g + 1) * rows]

    pairs = [list(range(k, min(k + 2, n - 1))) for k in range(0, n - 1, 2)]
    for index, pair in enumerate(pairs):
        for k in pair:
            make_block(k, targets[k])
        if index == 0:
            pl.semaphore_wait(barrier, n - 1 + nf - 1)
        for p in range(ng):
            for k in pair:
                send(p, k).start()
    make_block(n - 1, tile)

    u_load.wait()

    def apply_rows(pair, source):
        real, imag = pair[0], pair[1]
        left = jnp.concatenate(
            [jnp.concatenate([real, -imag], axis=1), jnp.concatenate([imag, real], axis=1)], axis=0
        )
        return lax.dot_general(
            left, u_buf[source], (((1,), (1,)), ((), ())), preferred_element_type=jnp.float32
        )

    half = n // 2
    arrivals = list(range(half, n - 1)) + list(range(half))
    for p in range(ng):
        total = apply_rows(sending[n - 1, group_of(p)], tile)
        for k in arrivals:
            arrival(p, k).wait_recv()
            total = total + apply_rows(landing[p, targets[k]], targets[k])
        spectrum = total.astype(jnp.bfloat16).reshape(2, gs, chunk, tile_rows)
        for c in range(gs):
            q = p * gs + c
            place = (freq + 1 + c) % gs
            part = spectrum[:, 0]
            for other in range(1, gs):
                part = jnp.where(place == other, spectrum[:, other], part)
            if q < nf - 1:
                spec_sending[q] = part
                spec_send(q).start()
            else:
                spec_out[freq] = part

    for q in range(nf - 1):
        p, c = q // gs, q % gs
        source = ((freq // gs + ng - 1 - p) % ng) * gs + (freq + 1 + c) % gs
        spec_arrival(q, source).wait_recv()
        spec_out[source] = spec_landing[source]
    for p in range(ng):
        for k in range(n - 1):
            send(p, k).wait_send()
    for q in range(nf - 1):
        spec_send(q).wait_send()


def shrink_kernel(nf, nt, spec, level, out, held, sems):
    rows, tile_rows = spec.shape[2], spec.shape[3]
    half = nt // 2
    scale = 1.0 / math.sqrt(nf)
    band = 16 if rows % 16 == 0 else rows
    lanes = 128

    def coefficient(func, f, t):
        value = func(2.0 * math.pi * ((f + 1) * t % nt) / nt)
        return 0.0 if abs(value) < 1e-12 else value * scale

    lane_v = lax.broadcasted_iota(jnp.int32, (rows, rows), 1)
    row_v = lax.broadcasted_iota(jnp.int32, (rows, rows), 0)
    square = jnp.broadcast_to(level[...] * level[...], (rows, rows))
    column = jnp.sum(jnp.where(lane_v == row_v, square, 0.0), axis=1, keepdims=True)
    squares = jnp.broadcast_to(column, (rows, lanes))
    copies = []
    for r in range(0, rows, band):
        lvl = squares[r:r + band, :]
        for l in range(0, tile_rows, lanes):
            values = [
                [spec[f, c, r:r + band, l:l + lanes].astype(jnp.float32) for c in range(2)]
                for f in range(nf)
            ]
            for t in range(half):
                sums = [None, None]
                for f in range(nf):
                    kind = (f + 1) % 2
                    terms = (
                        (coefficient(math.cos, f, t), values[f][0]),
                        (-coefficient(math.sin, f, t), values[f][1]),
                    )
                    for factor, value in terms:
                        if factor == 0.0:
                            continue
                        term = value * factor
                        sums[kind] = term if sums[kind] is None else sums[kind] + term
                even, odd = sums
                for place, signal in ((t, even + odd), (t + half, even - odd)):
                    power = signal * signal
                    held[place, r:r + band, l:l + lanes] = power * signal / (power + lvl)
        copy = pltpu.make_async_copy(
            held.at[:, pl.ds(r, band)], out.at[:, pl.ds(r, band)], sems.at[r // band]
        )
        copy.start()
        copies.append(copy)
    for copy in copies:
        copy.wait()


def body(n, nf, wavefield, column_bases, row_bases, tile_ranks, row_order, shrink_level):
    _, tile_rows, double_sources = wavefield.shape
    sources = double_sources // 2
    double_width = column_bases.shape[4]
    width = double_width // 2
    chunk = sources // nf
    nt = 3 * nf
    gs = 2 if nf % 2 == 0 else 1
    ng = nf // gs
    hbm = pl.BlockSpec(memory_space=pltpu.HBM)
    vmem = pl.BlockSpec(memory_space=pltpu.VMEM)
    bf16 = jnp.bfloat16
    tables = [pltpu.with_memory_space_constraint(a, pltpu.HBM) for a in (tile_ranks, row_order)]
    spec = pl.pallas_call(
        functools.partial(exchange_kernel, n, nf, gs),
        out_shape=jax.ShapeDtypeStruct((nf, 2, chunk, tile_rows), bf16),
        in_specs=[hbm] * 5,
        out_specs=vmem,
        scratch_shapes=[
            pltpu.VMEM((tile_rows, double_sources), bf16),
            pltpu.VMEM((n, tile_rows, double_width), bf16),
            pltpu.VMEM((n, tile_rows, double_width), bf16),
            pltpu.SMEM(tile_ranks.shape, jnp.int32),
            pltpu.SMEM(row_order.shape, jnp.int32),
            pltpu.VMEM((n, ng, 2, gs * chunk, width), bf16),
            pltpu.VMEM((ng, n, 2, gs * chunk, width), bf16),
            pltpu.VMEM((nf - 1, 2, chunk, tile_rows), bf16),
            pltpu.VMEM((nf, 2, chunk, tile_rows), bf16),
            pltpu.SemaphoreType.DMA((4,)),
            pltpu.SemaphoreType.DMA((n,)),
            pltpu.SemaphoreType.DMA((ng, n)),
            pltpu.SemaphoreType.DMA((ng, n)),
            pltpu.SemaphoreType.DMA((nf,)),
            pltpu.SemaphoreType.DMA((nf,)),
        ],
        compiler_params=pltpu.CompilerParams(
            collective_id=0, has_side_effects=True, vmem_limit_bytes=56_250_000
        ),
        name="exchange",
    )(wavefield, column_bases, row_bases, *tables)
    return pl.pallas_call(
        functools.partial(shrink_kernel, nf, nt),
        out_shape=jax.ShapeDtypeStruct((nt, chunk, tile_rows), jnp.float32),
        in_specs=[vmem, vmem],
        out_specs=hbm,
        scratch_shapes=[
            pltpu.VMEM((nt, chunk, tile_rows), jnp.float32),
            pltpu.SemaphoreType.DMA((max(1, chunk // 16),)),
        ],
        compiler_params=pltpu.CompilerParams(vmem_limit_bytes=16 * 1024 * 1024),
        name="shrink",
    )(spec, shrink_level[None])


def solution(mesh):
    in_specs = (
        P("freq", "tile", None),
        P("freq", "tile", None, None, None),
        P("freq", "tile", None, None, None),
        P(),
        P(),
        P("freq"),
    )
    out_specs = P(None, "freq", "tile")
    return jax.shard_map(
        functools.partial(body, mesh.shape["tile"], mesh.shape["freq"]),
        mesh=mesh, in_specs=in_specs, out_specs=out_specs, check_vma=False,
    )
```

```python
import functools
import math

import jax
import jax.numpy as jnp
from jax import lax
from jax.experimental import pallas as pl
from jax.experimental.pallas import tpu as pltpu
from jax.sharding import PartitionSpec as P

MESH = pl.DeviceIdType.MESH


def target(tile, k, n):
    half = n // 2
    late = tile // half
    inner = 0
    k = (k + half * inner) % (n - 1)
    turn = k - half
    near = turn + (turn + 2 * half - (tile - half * late)) // half - 1 + half * late
    far = k + half * (1 - late)
    is_near = k // half
    return near * is_near + far * (1 - is_near)


def exchange_kernel(n, nf, gs, wave, v_hbm, u_hbm, ranks_hbm, order_hbm,
                    spec_out,
                    x_buf, v_buf, u_buf, ranks, order, sending, landing,
                    spec_sending, spec_landing,
                    load_sems, v_sems, send_sems, recv_sems, spec_send_sems, spec_recv_sems):
    tile = lax.axis_index("tile")
    freq = lax.axis_index("freq")
    tile_rows = x_buf.shape[0]
    sources = x_buf.shape[1] // 2
    width = v_buf.shape[2] // 2
    chunk = sources // nf
    ng = nf // gs
    pieces = [(p * gs, gs) for p in range(ng - 1)] + [(q, 1) for q in range(nf - gs, nf)]
    targets = [target(tile, k, n) for k in range(n - 1)]
    half = n // 2
    far, near = list(range(half)), list(range(half, n - 1))
    F = lambda p: [(p, k) for k in far]
    N = lambda p: [(p, k) for k in near]
    plan = F(0)+N(0)+N(1)+N(2)+[(1,0),(2,0),(1,1),(2,1),(1,2),(1,3),(2,2),(2,3)]

    loads = [
        pltpu.make_async_copy(wave.at[0], x_buf, load_sems.at[0]),
        pltpu.make_async_copy(ranks_hbm, ranks, load_sems.at[2]),
        pltpu.make_async_copy(order_hbm, order, load_sems.at[3]),
    ]
    v_loads = [pltpu.make_async_copy(v_hbm.at[0, 0, i], v_buf.at[i], v_sems.at[i]) for i in range(n)]
    u_load = pltpu.make_async_copy(u_hbm.at[0, 0], u_buf, load_sems.at[1])
    for load in loads + v_loads:
        load.start()

    barrier = pltpu.get_barrier_semaphore()
    for other in targets:
        pl.semaphore_signal(barrier, inc=1, device_id={"tile": other}, device_id_type=MESH)
    for hop in range(1, nf):
        pl.semaphore_signal(
            barrier, inc=1, device_id={"freq": (freq + hop) % nf}, device_id_type=MESH
        )

    def receiver_of(q):
        group = (freq // gs + 1 + q // gs) % ng
        return group * gs + (q % gs if q < nf - gs else (freq + 1 + q) % gs)

    def send(p, k):
        q, count = pieces[p]
        return pltpu.make_async_remote_copy(
            src_ref=sending.at[k, pl.ds(receiver_of(q), count)],
            dst_ref=landing.at[tile, pl.ds(q, count)],
            send_sem=send_sems.at[p, k],
            recv_sem=recv_sems.at[p, tile],
            device_id={"tile": targets[k]},
            device_id_type=MESH,
        )

    def arrival(p, k):
        q, count = pieces[p]
        return pltpu.make_async_remote_copy(
            src_ref=sending.at[k, pl.ds(receiver_of(q), count)],
            dst_ref=landing.at[targets[k], pl.ds(q, count)],
            send_sem=send_sems.at[p, k],
            recv_sem=recv_sems.at[p, targets[k]],
            device_id={"tile": targets[k]},
            device_id_type=MESH,
        )

    def spec_send(q):
        return pltpu.make_async_remote_copy(
            src_ref=spec_sending.at[q],
            dst_ref=spec_landing.at[freq],
            send_sem=spec_send_sems.at[q],
            recv_sem=spec_recv_sems.at[freq],
            device_id={"freq": receiver_of(q)},
            device_id_type=MESH,
        )

    def spec_arrival(q, source):
        return pltpu.make_async_remote_copy(
            src_ref=spec_sending.at[q],
            dst_ref=spec_landing.at[source],
            send_sem=spec_send_sems.at[q],
            recv_sem=spec_recv_sems.at[source],
            device_id={"freq": receiver_of(q)},
            device_id_type=MESH,
        )

    for load in loads:
        load.wait()
    x_t = x_buf[...].T
    for load in v_loads:
        load.wait()
    u_load.start()

    lane = lax.broadcasted_iota(jnp.int32, (sources, width), 1)

    def make_block(k, slot):
        row = order[slot]
        rank = ranks[row, tile]
        product = jnp.dot(x_t, v_buf[row], preferred_element_type=jnp.float32)
        keep = lane < rank
        real = product[:sources, :width] + product[sources:, width:]
        imag = product[sources:, :width] - product[:sources, width:]
        real = jnp.where(keep, real, 0.0).astype(jnp.bfloat16)
        imag = jnp.where(keep, imag, 0.0).astype(jnp.bfloat16)
        for c in range(nf):
            sending[k, c, 0] = real[c * chunk:(c + 1) * chunk]
            sending[k, c, 1] = imag[c * chunk:(c + 1) * chunk]

    made = set()

    def make(k):
        if k not in made:
            made.add(k)
            make_block(k, targets[k])

    for index, (p, k) in enumerate(plan):
        make(k)
        if index == 0:
            pl.semaphore_wait(barrier, n - 1 + nf - 1)
        elif index + 1 < len(plan):
            make(plan[index + 1][1])
        send(p, k).start()
    make_block(n - 1, tile)

    u_load.wait()

    def apply_rows(piece, source):
        real, imag = (piece[:, c].reshape(-1, width) for c in range(2))
        left = jnp.concatenate(
            [jnp.concatenate([real, -imag], axis=1), jnp.concatenate([imag, real], axis=1)], axis=0
        )
        return lax.dot_general(
            left, u_buf[source], (((1,), (1,)), ((), ())), preferred_element_type=jnp.float32
        )

    arrivals = near + far
    for p, (first, count) in enumerate(pieces):
        total = apply_rows(sending[n - 1, pl.ds(receiver_of(first), count)], tile)
        for k in arrivals:
            arrival(p, k).wait_recv()
            total = total + apply_rows(landing[targets[k], pl.ds(first, count)], targets[k])
        spectrum = total.astype(jnp.bfloat16).reshape(2, count, chunk, tile_rows)
        for c in range(count):
            if first + c < nf - 1:
                spec_sending[first + c] = spectrum[:, c]
                spec_send(first + c).start()
            else:
                spec_out[freq] = spectrum[:, c]

    for q in range(nf - 1):
        group = (freq // gs + ng - 1 - q // gs) % ng
        if q < nf - gs:
            sources_of = [group * gs + c for c in range(gs)] if q % gs == 0 else []
        else:
            sources_of = [group * gs + (freq + nf - 1 - q) % gs]
        for source in sources_of:
            spec_arrival(q, source).wait_recv()
            spec_out[source] = spec_landing[source]
    for p in range(len(pieces)):
        for k in range(n - 1):
            send(p, k).wait_send()
    for q in range(nf - 1):
        spec_send(q).wait_send()


def shrink_kernel(nf, nt, spec, level, out, held, sems):
    rows, tile_rows = spec.shape[2], spec.shape[3]
    half = nt // 2
    scale = 1.0 / math.sqrt(nf)
    band = 16 if rows % 16 == 0 else rows
    lanes = 128

    def coefficient(func, f, t):
        value = func(2.0 * math.pi * ((f + 1) * t % nt) / nt)
        return 0.0 if abs(value) < 1e-12 else value * scale

    lane_v = lax.broadcasted_iota(jnp.int32, (rows, rows), 1)
    row_v = lax.broadcasted_iota(jnp.int32, (rows, rows), 0)
    square = jnp.broadcast_to(level[...] * level[...], (rows, rows))
    column = jnp.sum(jnp.where(lane_v == row_v, square, 0.0), axis=1, keepdims=True)
    squares = jnp.broadcast_to(column, (rows, lanes))
    copies = []
    for r in range(0, rows, band):
        lvl = squares[r:r + band, :]
        for l in range(0, tile_rows, lanes):
            values = [
                [spec[f, c, r:r + band, l:l + lanes].astype(jnp.float32) for c in range(2)]
                for f in range(nf)
            ]
            for t in range(half):
                sums = [None, None]
                for f in range(nf):
                    kind = (f + 1) % 2
                    terms = (
                        (coefficient(math.cos, f, t), values[f][0]),
                        (-coefficient(math.sin, f, t), values[f][1]),
                    )
                    for factor, value in terms:
                        if factor == 0.0:
                            continue
                        term = value * factor
                        sums[kind] = term if sums[kind] is None else sums[kind] + term
                even, odd = sums
                for place, signal in ((t, even + odd), (t + half, even - odd)):
                    power = signal * signal
                    held[place, r:r + band, l:l + lanes] = power * signal / (power + lvl)
        copy = pltpu.make_async_copy(
            held.at[:, pl.ds(r, band)], out.at[:, pl.ds(r, band)], sems.at[r // band]
        )
        copy.start()
        copies.append(copy)
    for copy in copies:
        copy.wait()


def body(n, nf, wavefield, column_bases, row_bases, tile_ranks, row_order, shrink_level):
    _, tile_rows, double_sources = wavefield.shape
    sources = double_sources // 2
    double_width = column_bases.shape[4]
    width = double_width // 2
    chunk = sources // nf
    nt = 3 * nf
    gs = 2 if nf % 2 == 0 else 1
    ng = nf // gs
    hbm = pl.BlockSpec(memory_space=pltpu.HBM)
    vmem = pl.BlockSpec(memory_space=pltpu.VMEM)
    bf16 = jnp.bfloat16
    tables = [pltpu.with_memory_space_constraint(a, pltpu.HBM) for a in (tile_ranks, row_order)]
    spec = pl.pallas_call(
        functools.partial(exchange_kernel, n, nf, gs),
        out_shape=jax.ShapeDtypeStruct((nf, 2, chunk, tile_rows), bf16),
        in_specs=[hbm] * 5,
        out_specs=vmem,
        scratch_shapes=[
            pltpu.VMEM((tile_rows, double_sources), bf16),
            pltpu.VMEM((n, tile_rows, double_width), bf16),
            pltpu.VMEM((n, tile_rows, double_width), bf16),
            pltpu.SMEM(tile_ranks.shape, jnp.int32),
            pltpu.SMEM(row_order.shape, jnp.int32),
            pltpu.VMEM((n, nf, 2, chunk, width), bf16),
            pltpu.VMEM((n, nf, 2, chunk, width), bf16),
            pltpu.VMEM((nf - 1, 2, chunk, tile_rows), bf16),
            pltpu.VMEM((nf, 2, chunk, tile_rows), bf16),
            pltpu.SemaphoreType.DMA((4,)),
            pltpu.SemaphoreType.DMA((n,)),
            pltpu.SemaphoreType.DMA((ng - 1 + gs, n)),
            pltpu.SemaphoreType.DMA((ng - 1 + gs, n)),
            pltpu.SemaphoreType.DMA((nf,)),
            pltpu.SemaphoreType.DMA((nf,)),
        ],
        compiler_params=pltpu.CompilerParams(
            collective_id=0, has_side_effects=True, vmem_limit_bytes=56_250_000
        ),
        name="exchange",
    )(wavefield, column_bases, row_bases, *tables)
    return pl.pallas_call(
        functools.partial(shrink_kernel, nf, nt),
        out_shape=jax.ShapeDtypeStruct((nt, chunk, tile_rows), jnp.float32),
        in_specs=[vmem, vmem],
        out_specs=hbm,
        scratch_shapes=[
            pltpu.VMEM((nt, chunk, tile_rows), jnp.float32),
            pltpu.SemaphoreType.DMA((max(1, chunk // 16),)),
        ],
        compiler_params=pltpu.CompilerParams(vmem_limit_bytes=16 * 1024 * 1024),
        name="shrink",
    )(spec, shrink_level[None])


def solution(mesh):
    in_specs = (
        P("freq", "tile", None),
        P("freq", "tile", None, None, None),
        P("freq", "tile", None, None, None),
        P(),
        P(),
        P("freq"),
    )
    out_specs = P(None, "freq", "tile")
    return jax.shard_map(
        functools.partial(body, mesh.shape["tile"], mesh.shape["freq"]),
        mesh=mesh, in_specs=in_specs, out_specs=out_specs, check_vma=False,
    )
```

```python
import functools
import math

import jax
import jax.numpy as jnp
from jax import lax
from jax.experimental import pallas as pl
from jax.experimental.pallas import tpu as pltpu
from jax.sharding import PartitionSpec as P

MESH = pl.DeviceIdType.MESH


def target(tile, k, n):
    half = n // 2
    late = tile // half
    place = tile * late + (n - 1 - tile) * (1 - late)
    other = k + (k + n - place) // n
    return other * late + (n - 1 - other) * (1 - late)


def exchange_kernel(n, nf, gs, wave, v_hbm, u_hbm, ranks_hbm, order_hbm,
                    spec_out,
                    x_buf, v_buf, u_buf, ranks, order, sending, landing,
                    spec_sending, spec_landing,
                    load_sems, v_sems, send_sems, recv_sems, spec_send_sems, spec_recv_sems):
    tile = lax.axis_index("tile")
    freq = lax.axis_index("freq")
    tile_rows = x_buf.shape[0]
    sources = x_buf.shape[1] // 2
    width = v_buf.shape[2] // 2
    chunk = sources // nf
    ng = nf // gs
    pieces = [(p * gs, gs) for p in range(ng - 1)] + [(q, 1) for q in range(nf - gs, nf)]
    targets = [target(tile, k, n) for k in range(n - 1)]
    half = n // 2
    far, near = list(range(half)), list(range(half, n - 1))
    later = range(1, len(pieces))
    plan = [(0, k) for k in far[:half // 2]]
    plan += [(p, k) for k in near for p in range(len(pieces))]
    plan += [(0, k) for k in far[half // 2:]]
    plan += [(p, k) for k in far for p in later]

    loads = [
        pltpu.make_async_copy(wave.at[0], x_buf, load_sems.at[0]),
        pltpu.make_async_copy(ranks_hbm, ranks, load_sems.at[2]),
        pltpu.make_async_copy(order_hbm, order, load_sems.at[3]),
    ]
    v_loads = [pltpu.make_async_copy(v_hbm.at[0, 0, i], v_buf.at[i], v_sems.at[i]) for i in range(n)]
    u_load = pltpu.make_async_copy(u_hbm.at[0, 0], u_buf, load_sems.at[1])
    for load in loads + v_loads:
        load.start()

    barrier = pltpu.get_barrier_semaphore()
    for other in targets:
        pl.semaphore_signal(barrier, inc=1, device_id={"tile": other}, device_id_type=MESH)
    for hop in range(1, nf):
        pl.semaphore_signal(
            barrier, inc=1, device_id={"freq": (freq + hop) % nf}, device_id_type=MESH
        )

    def receiver_of(q):
        group = (freq // gs + 1 + q // gs) % ng
        return group * gs + (q % gs if q < nf - gs else (freq + 1 + q) % gs)

    def send(p, k):
        q, count = pieces[p]
        return pltpu.make_async_remote_copy(
            src_ref=sending.at[k, pl.ds(receiver_of(q), count)],
            dst_ref=landing.at[tile, pl.ds(q, count)],
            send_sem=send_sems.at[p, k],
            recv_sem=recv_sems.at[p, tile],
            device_id={"tile": targets[k]},
            device_id_type=MESH,
        )

    def arrival(p, k):
        q, count = pieces[p]
        return pltpu.make_async_remote_copy(
            src_ref=sending.at[k, pl.ds(receiver_of(q), count)],
            dst_ref=landing.at[targets[k], pl.ds(q, count)],
            send_sem=send_sems.at[p, k],
            recv_sem=recv_sems.at[p, targets[k]],
            device_id={"tile": targets[k]},
            device_id_type=MESH,
        )

    def spec_send(q):
        return pltpu.make_async_remote_copy(
            src_ref=spec_sending.at[q],
            dst_ref=spec_landing.at[freq],
            send_sem=spec_send_sems.at[q],
            recv_sem=spec_recv_sems.at[freq],
            device_id={"freq": receiver_of(q)},
            device_id_type=MESH,
        )

    def spec_arrival(q, source):
        return pltpu.make_async_remote_copy(
            src_ref=spec_sending.at[q],
            dst_ref=spec_landing.at[source],
            send_sem=spec_send_sems.at[q],
            recv_sem=spec_recv_sems.at[source],
            device_id={"freq": receiver_of(q)},
            device_id_type=MESH,
        )

    for load in loads:
        load.wait()
    x_t = x_buf[...].T
    for load in v_loads:
        load.wait()
    u_load.start()

    lane = lax.broadcasted_iota(jnp.int32, (sources, width), 1)

    def make_block(k, slot):
        row = order[slot]
        rank = ranks[row, tile]
        product = jnp.dot(x_t, v_buf[row], preferred_element_type=jnp.float32)
        keep = lane < rank
        real = product[:sources, :width] + product[sources:, width:]
        imag = product[sources:, :width] - product[:sources, width:]
        real = jnp.where(keep, real, 0.0).astype(jnp.bfloat16)
        imag = jnp.where(keep, imag, 0.0).astype(jnp.bfloat16)
        for c in range(nf):
            sending[k, c, 0] = real[c * chunk:(c + 1) * chunk]
            sending[k, c, 1] = imag[c * chunk:(c + 1) * chunk]

    made = set()

    def make(k):
        if k not in made:
            made.add(k)
            make_block(k, targets[k])

    for index, (p, k) in enumerate(plan):
        make(k)
        if index == 0:
            pl.semaphore_wait(barrier, n - 1 + nf - 1)
        elif index + 1 < len(plan):
            make(plan[index + 1][1])
        send(p, k).start()
    make_block(n - 1, tile)

    u_load.wait()

    def apply_rows(piece, source):
        real, imag = (piece[:, c].reshape(-1, width) for c in range(2))
        left = jnp.concatenate(
            [jnp.concatenate([real, -imag], axis=1), jnp.concatenate([imag, real], axis=1)], axis=0
        )
        return lax.dot_general(
            left, u_buf[source], (((1,), (1,)), ((), ())), preferred_element_type=jnp.float32
        )

    arrivals = near + far
    for p, (first, count) in enumerate(pieces):
        total = apply_rows(sending[n - 1, pl.ds(receiver_of(first), count)], tile)
        for k in arrivals:
            arrival(p, k).wait_recv()
            total = total + apply_rows(landing[targets[k], pl.ds(first, count)], targets[k])
        spectrum = total.astype(jnp.bfloat16).reshape(2, count, chunk, tile_rows)
        for c in range(count):
            if first + c < nf - 1:
                spec_sending[first + c] = spectrum[:, c]
                spec_send(first + c).start()
            else:
                spec_out[freq] = spectrum[:, c]

    for q in range(nf - 1):
        group = (freq // gs + ng - 1 - q // gs) % ng
        if q < nf - gs:
            sources_of = [group * gs + c for c in range(gs)] if q % gs == 0 else []
        else:
            sources_of = [group * gs + (freq + nf - 1 - q) % gs]
        for source in sources_of:
            spec_arrival(q, source).wait_recv()
            spec_out[source] = spec_landing[source]
    for p in range(len(pieces)):
        for k in range(n - 1):
            send(p, k).wait_send()
    for q in range(nf - 1):
        spec_send(q).wait_send()


def shrink_kernel(nf, nt, spec, level, out, held, sems):
    rows, tile_rows = spec.shape[2], spec.shape[3]
    half = nt // 2
    scale = 1.0 / math.sqrt(nf)
    band = 16 if rows % 16 == 0 else rows
    lanes = 128

    def coefficient(func, f, t):
        value = func(2.0 * math.pi * ((f + 1) * t % nt) / nt)
        return 0.0 if abs(value) < 1e-12 else value * scale

    lane_v = lax.broadcasted_iota(jnp.int32, (rows, rows), 1)
    row_v = lax.broadcasted_iota(jnp.int32, (rows, rows), 0)
    square = jnp.broadcast_to(level[...] * level[...], (rows, rows))
    column = jnp.sum(jnp.where(lane_v == row_v, square, 0.0), axis=1, keepdims=True)
    squares = jnp.broadcast_to(column, (rows, lanes))
    copies = []
    for r in range(0, rows, band):
        lvl = squares[r:r + band, :]
        for l in range(0, tile_rows, lanes):
            values = [
                [spec[f, c, r:r + band, l:l + lanes].astype(jnp.float32) for c in range(2)]
                for f in range(nf)
            ]
            for t in range(half):
                sums = [None, None]
                for f in range(nf):
                    kind = (f + 1) % 2
                    terms = (
                        (coefficient(math.cos, f, t), values[f][0]),
                        (-coefficient(math.sin, f, t), values[f][1]),
                    )
                    for factor, value in terms:
                        if factor == 0.0:
                            continue
                        term = value * factor
                        sums[kind] = term if sums[kind] is None else sums[kind] + term
                even, odd = sums
                for place, signal in ((t, even + odd), (t + half, even - odd)):
                    power = signal * signal
                    held[place, r:r + band, l:l + lanes] = power * signal / (power + lvl)
        copy = pltpu.make_async_copy(
            held.at[:, pl.ds(r, band)], out.at[:, pl.ds(r, band)], sems.at[r // band]
        )
        copy.start()
        copies.append(copy)
    for copy in copies:
        copy.wait()


def body(n, nf, wavefield, column_bases, row_bases, tile_ranks, row_order, shrink_level):
    _, tile_rows, double_sources = wavefield.shape
    sources = double_sources // 2
    double_width = column_bases.shape[4]
    width = double_width // 2
    chunk = sources // nf
    nt = 3 * nf
    gs = 2 if nf % 2 == 0 else 1
    ng = nf // gs
    hbm = pl.BlockSpec(memory_space=pltpu.HBM)
    vmem = pl.BlockSpec(memory_space=pltpu.VMEM)
    bf16 = jnp.bfloat16
    tables = [pltpu.with_memory_space_constraint(a, pltpu.HBM) for a in (tile_ranks, row_order)]
    spec = pl.pallas_call(
        functools.partial(exchange_kernel, n, nf, gs),
        out_shape=jax.ShapeDtypeStruct((nf, 2, chunk, tile_rows), bf16),
        in_specs=[hbm] * 5,
        out_specs=vmem,
        scratch_shapes=[
            pltpu.VMEM((tile_rows, double_sources), bf16),
            pltpu.VMEM((n, tile_rows, double_width), bf16),
            pltpu.VMEM((n, tile_rows, double_width), bf16),
            pltpu.SMEM(tile_ranks.shape, jnp.int32),
            pltpu.SMEM(row_order.shape, jnp.int32),
            pltpu.VMEM((n, nf, 2, chunk, width), bf16),
            pltpu.VMEM((n, nf, 2, chunk, width), bf16),
            pltpu.VMEM((nf - 1, 2, chunk, tile_rows), bf16),
            pltpu.VMEM((nf, 2, chunk, tile_rows), bf16),
            pltpu.SemaphoreType.DMA((4,)),
            pltpu.SemaphoreType.DMA((n,)),
            pltpu.SemaphoreType.DMA((ng - 1 + gs, n)),
            pltpu.SemaphoreType.DMA((ng - 1 + gs, n)),
            pltpu.SemaphoreType.DMA((nf,)),
            pltpu.SemaphoreType.DMA((nf,)),
        ],
        compiler_params=pltpu.CompilerParams(
            collective_id=0, has_side_effects=True, vmem_limit_bytes=56_250_000
        ),
        name="exchange",
    )(wavefield, column_bases, row_bases, *tables)
    return pl.pallas_call(
        functools.partial(shrink_kernel, nf, nt),
        out_shape=jax.ShapeDtypeStruct((nt, chunk, tile_rows), jnp.float32),
        in_specs=[vmem, vmem],
        out_specs=hbm,
        scratch_shapes=[
            pltpu.VMEM((nt, chunk, tile_rows), jnp.float32),
            pltpu.SemaphoreType.DMA((max(1, chunk // 16),)),
        ],
        compiler_params=pltpu.CompilerParams(vmem_limit_bytes=16 * 1024 * 1024),
        name="shrink",
    )(spec, shrink_level[None])


def solution(mesh):
    in_specs = (
        P("freq", "tile", None),
        P("freq", "tile", None, None, None),
        P("freq", "tile", None, None, None),
        P(),
        P(),
        P("freq"),
    )
    out_specs = P(None, "freq", "tile")
    return jax.shard_map(
        functools.partial(body, mesh.shape["tile"], mesh.shape["freq"]),
        mesh=mesh, in_specs=in_specs, out_specs=out_specs, check_vma=False,
    )
```

```python
import functools
import math

import jax
import jax.numpy as jnp
from jax import lax
from jax.experimental import pallas as pl
from jax.experimental.pallas import tpu as pltpu
from jax.sharding import PartitionSpec as P

MESH = pl.DeviceIdType.MESH


def target(tile, k, n):
    half = n // 2
    late = tile // half
    place = tile * late + (n - 1 - tile) * (1 - late)
    other = k + (k + n - place) // n
    return other * late + (n - 1 - other) * (1 - late)


def exchange_kernel(n, nf, gs, wave, v_hbm, u_hbm, ranks_hbm, order_hbm,
                    spec_out,
                    x_buf, v_buf, u_buf, ranks, order, sending, landing,
                    spec_sending, spec_landing,
                    load_sems, v_sems, send_sems, recv_sems, spec_send_sems, spec_recv_sems):
    tile = lax.axis_index("tile")
    freq = lax.axis_index("freq")
    tile_rows = x_buf.shape[0]
    sources = x_buf.shape[1] // 2
    width = v_buf.shape[2] // 2
    chunk = sources // nf
    ng = nf // gs
    pieces = [(p * gs, gs) for p in range(ng - 1)] + [(q, 1) for q in range(nf - gs, nf)]
    targets = [target(tile, k, n) for k in range(n - 1)]
    half = n // 2
    far, near = list(range(half)), list(range(half, n - 1))
    later = range(1, len(pieces))
    plan = [(0, k) for k in far[:half // 2]]
    plan += [(p, k) for k in near for p in range(len(pieces))]
    plan += [(0, k) for k in far[half // 2:]]
    plan += [(p, k) for k in far for p in later]

    loads = [
        pltpu.make_async_copy(wave.at[0], x_buf, load_sems.at[0]),
        pltpu.make_async_copy(ranks_hbm, ranks, load_sems.at[2]),
        pltpu.make_async_copy(order_hbm, order, load_sems.at[3]),
    ]
    v_loads = [pltpu.make_async_copy(v_hbm.at[0, 0, i], v_buf.at[i], v_sems.at[i]) for i in range(n)]
    u_load = pltpu.make_async_copy(u_hbm.at[0, 0], u_buf, load_sems.at[1])
    for load in loads + v_loads:
        load.start()

    barrier = pltpu.get_barrier_semaphore()
    for other in targets:
        pl.semaphore_signal(barrier, inc=1, device_id={"tile": other}, device_id_type=MESH)
    for hop in range(1, nf):
        pl.semaphore_signal(
            barrier, inc=1, device_id={"freq": (freq + hop) % nf}, device_id_type=MESH
        )

    def receiver_of(q):
        group = (freq // gs + 1 + q // gs) % ng
        return group * gs + (q % gs if q < nf - gs else (freq + 1 + q) % gs)

    def send(p, k):
        q, count = pieces[p]
        return pltpu.make_async_remote_copy(
            src_ref=sending.at[k, pl.ds(receiver_of(q), count)],
            dst_ref=landing.at[tile, pl.ds(q, count)],
            send_sem=send_sems.at[p, k],
            recv_sem=recv_sems.at[p, tile],
            device_id={"tile": targets[k]},
            device_id_type=MESH,
        )

    def arrival(p, k):
        q, count = pieces[p]
        return pltpu.make_async_remote_copy(
            src_ref=sending.at[k, pl.ds(receiver_of(q), count)],
            dst_ref=landing.at[targets[k], pl.ds(q, count)],
            send_sem=send_sems.at[p, k],
            recv_sem=recv_sems.at[p, targets[k]],
            device_id={"tile": targets[k]},
            device_id_type=MESH,
        )

    def spec_send(q):
        return pltpu.make_async_remote_copy(
            src_ref=spec_sending.at[q],
            dst_ref=spec_landing.at[freq],
            send_sem=spec_send_sems.at[q],
            recv_sem=spec_recv_sems.at[freq],
            device_id={"freq": receiver_of(q)},
            device_id_type=MESH,
        )

    def spec_arrival(q, source):
        return pltpu.make_async_remote_copy(
            src_ref=spec_sending.at[q],
            dst_ref=spec_landing.at[source],
            send_sem=spec_send_sems.at[q],
            recv_sem=spec_recv_sems.at[source],
            device_id={"freq": receiver_of(q)},
            device_id_type=MESH,
        )

    for load in loads:
        load.wait()
    x_t = x_buf[...].T
    for load in v_loads:
        load.wait()
    u_load.start()

    lane = lax.broadcasted_iota(jnp.int32, (sources, width), 1)

    def make_block(k, slot):
        row = order[slot]
        rank = ranks[row, tile]
        product = jnp.dot(x_t, v_buf[row], preferred_element_type=jnp.float32)
        keep = lane < rank
        real = product[:sources, :width] + product[sources:, width:]
        imag = product[sources:, :width] - product[:sources, width:]
        real = jnp.where(keep, real, 0.0).astype(jnp.bfloat16)
        imag = jnp.where(keep, imag, 0.0).astype(jnp.bfloat16)
        for c in range(nf):
            sending[k, c, 0] = real[c * chunk:(c + 1) * chunk]
            sending[k, c, 1] = imag[c * chunk:(c + 1) * chunk]

    made = set()

    def make(k):
        if k not in made:
            made.add(k)
            make_block(k, targets[k])

    for index, (p, k) in enumerate(plan):
        make(k)
        if index == 0:
            pl.semaphore_wait(barrier, n - 1 + nf - 1)
        elif index + 1 < len(plan):
            make(plan[index + 1][1])
        send(p, k).start()
    make_block(n - 1, tile)

    u_load.wait()

    def apply_rows(piece, source):
        real, imag = (piece[:, c].reshape(-1, width) for c in range(2))
        left = jnp.concatenate(
            [jnp.concatenate([real, -imag], axis=1), jnp.concatenate([imag, real], axis=1)], axis=0
        )
        return lax.dot_general(
            left, u_buf[source], (((1,), (1,)), ((), ())), preferred_element_type=jnp.float32
        )

    arrivals = near[::-1] + far
    for p, (first, count) in enumerate(pieces):
        total = apply_rows(sending[n - 1, pl.ds(receiver_of(first), count)], tile)
        for k in arrivals:
            arrival(p, k).wait_recv()
            total = total + apply_rows(landing[targets[k], pl.ds(first, count)], targets[k])
        spectrum = total.astype(jnp.bfloat16).reshape(2, count, chunk, tile_rows)
        for c in range(count):
            if first + c < nf - 1:
                spec_sending[first + c] = spectrum[:, c]
                spec_send(first + c).start()
            else:
                spec_out[freq] = spectrum[:, c]

    for q in range(nf - 1):
        group = (freq // gs + ng - 1 - q // gs) % ng
        if q < nf - gs:
            sources_of = [group * gs + c for c in range(gs)] if q % gs == 0 else []
        else:
            sources_of = [group * gs + (freq + nf - 1 - q) % gs]
        for source in sources_of:
            spec_arrival(q, source).wait_recv()
            spec_out[source] = spec_landing[source]
    for p in range(len(pieces)):
        for k in range(n - 1):
            send(p, k).wait_send()
    for q in range(nf - 1):
        spec_send(q).wait_send()


def shrink_kernel(nf, nt, spec, level, out, held, sems):
    rows, tile_rows = spec.shape[2], spec.shape[3]
    half = nt // 2
    scale = 1.0 / math.sqrt(nf)
    band = 16 if rows % 16 == 0 else rows
    lanes = 128

    def coefficient(func, f, t):
        value = func(2.0 * math.pi * ((f + 1) * t % nt) / nt)
        return 0.0 if abs(value) < 1e-12 else value * scale

    lane_v = lax.broadcasted_iota(jnp.int32, (rows, rows), 1)
    row_v = lax.broadcasted_iota(jnp.int32, (rows, rows), 0)
    square = jnp.broadcast_to(level[...] * level[...], (rows, rows))
    column = jnp.sum(jnp.where(lane_v == row_v, square, 0.0), axis=1, keepdims=True)
    squares = jnp.broadcast_to(column, (rows, lanes))
    copies = []
    for r in range(0, rows, band):
        lvl = squares[r:r + band, :]
        for l in range(0, tile_rows, lanes):
            values = [
                [spec[f, c, r:r + band, l:l + lanes].astype(jnp.float32) for c in range(2)]
                for f in range(nf)
            ]
            for t in range(half):
                sums = [None, None]
                for f in range(nf):
                    kind = (f + 1) % 2
                    terms = (
                        (coefficient(math.cos, f, t), values[f][0]),
                        (-coefficient(math.sin, f, t), values[f][1]),
                    )
                    for factor, value in terms:
                        if factor == 0.0:
                            continue
                        term = value * factor
                        sums[kind] = term if sums[kind] is None else sums[kind] + term
                even, odd = sums
                for place, signal in ((t, even + odd), (t + half, even - odd)):
                    power = signal * signal
                    held[place, r:r + band, l:l + lanes] = power * signal / (power + lvl)
        copy = pltpu.make_async_copy(
            held.at[:, pl.ds(r, band)], out.at[:, pl.ds(r, band)], sems.at[r // band]
        )
        copy.start()
        copies.append(copy)
    for copy in copies:
        copy.wait()


def body(n, nf, wavefield, column_bases, row_bases, tile_ranks, row_order, shrink_level):
    _, tile_rows, double_sources = wavefield.shape
    sources = double_sources // 2
    double_width = column_bases.shape[4]
    width = double_width // 2
    chunk = sources // nf
    nt = 3 * nf
    gs = 2 if nf % 2 == 0 else 1
    ng = nf // gs
    hbm = pl.BlockSpec(memory_space=pltpu.HBM)
    vmem = pl.BlockSpec(memory_space=pltpu.VMEM)
    bf16 = jnp.bfloat16
    tables = [pltpu.with_memory_space_constraint(a, pltpu.HBM) for a in (tile_ranks, row_order)]
    spec = pl.pallas_call(
        functools.partial(exchange_kernel, n, nf, gs),
        out_shape=jax.ShapeDtypeStruct((nf, 2, chunk, tile_rows), bf16),
        in_specs=[hbm] * 5,
        out_specs=vmem,
        scratch_shapes=[
            pltpu.VMEM((tile_rows, double_sources), bf16),
            pltpu.VMEM((n, tile_rows, double_width), bf16),
            pltpu.VMEM((n, tile_rows, double_width), bf16),
            pltpu.SMEM(tile_ranks.shape, jnp.int32),
            pltpu.SMEM(row_order.shape, jnp.int32),
            pltpu.VMEM((n, nf, 2, chunk, width), bf16),
            pltpu.VMEM((n, nf, 2, chunk, width), bf16),
            pltpu.VMEM((nf - 1, 2, chunk, tile_rows), bf16),
            pltpu.VMEM((nf, 2, chunk, tile_rows), bf16),
            pltpu.SemaphoreType.DMA((4,)),
            pltpu.SemaphoreType.DMA((n,)),
            pltpu.SemaphoreType.DMA((ng - 1 + gs, n)),
            pltpu.SemaphoreType.DMA((ng - 1 + gs, n)),
            pltpu.SemaphoreType.DMA((nf,)),
            pltpu.SemaphoreType.DMA((nf,)),
        ],
        compiler_params=pltpu.CompilerParams(
            collective_id=0, has_side_effects=True, vmem_limit_bytes=56_250_000
        ),
        name="exchange",
    )(wavefield, column_bases, row_bases, *tables)
    return pl.pallas_call(
        functools.partial(shrink_kernel, nf, nt),
        out_shape=jax.ShapeDtypeStruct((nt, chunk, tile_rows), jnp.float32),
        in_specs=[vmem, vmem],
        out_specs=hbm,
        scratch_shapes=[
            pltpu.VMEM((nt, chunk, tile_rows), jnp.float32),
            pltpu.SemaphoreType.DMA((max(1, chunk // 16),)),
        ],
        compiler_params=pltpu.CompilerParams(vmem_limit_bytes=16 * 1024 * 1024),
        name="shrink",
    )(spec, shrink_level[None])


def solution(mesh):
    in_specs = (
        P("freq", "tile", None),
        P("freq", "tile", None, None, None),
        P("freq", "tile", None, None, None),
        P(),
        P(),
        P("freq"),
    )
    out_specs = P(None, "freq", "tile")
    return jax.shard_map(
        functools.partial(body, mesh.shape["tile"], mesh.shape["freq"]),
        mesh=mesh, in_specs=in_specs, out_specs=out_specs, check_vma=False,
    )
```

```python
import functools
import math

import jax
import jax.numpy as jnp
from jax import lax
from jax.experimental import pallas as pl
from jax.experimental.pallas import tpu as pltpu
from jax.sharding import PartitionSpec as P

MESH = pl.DeviceIdType.MESH


def target(tile, k, n):
    half = n // 2
    late = tile // half
    place = tile * late + (n - 1 - tile) * (1 - late)
    other = k + (k + n - place) // n
    return other * late + (n - 1 - other) * (1 - late)


def exchange_kernel(n, nf, gs, wave, v_hbm, u_hbm, ranks_hbm, order_hbm,
                    spec_out,
                    x_buf, v_buf, u_buf, ranks, order, sending, landing,
                    spec_sending, spec_landing,
                    load_sems, v_sems, send_sems, recv_sems, spec_send_sems, spec_recv_sems):
    tile = lax.axis_index("tile")
    freq = lax.axis_index("freq")
    tile_rows = x_buf.shape[0]
    sources = x_buf.shape[1] // 2
    width = v_buf.shape[2] // 2
    chunk = sources // nf
    ng = nf // gs
    pieces = [(p * gs, gs) for p in range(ng - 1)] + [(q, 1) for q in range(nf - gs, nf)]
    targets = [target(tile, k, n) for k in range(n - 1)]
    half = n // 2
    far, near = list(range(half)), list(range(half, n - 1))
    later = range(1, len(pieces))
    plan = [(0, k) for k in far[:half // 2]]
    plan += [(p, k) for k in near for p in range(len(pieces))]
    plan += [(0, k) for k in far[half // 2:]]
    plan += [(p, k) for k in far for p in later]

    loads = [
        pltpu.make_async_copy(wave.at[0], x_buf, load_sems.at[0]),
        pltpu.make_async_copy(ranks_hbm, ranks, load_sems.at[2]),
        pltpu.make_async_copy(order_hbm, order, load_sems.at[3]),
    ]
    v_loads = [pltpu.make_async_copy(v_hbm.at[0, 0, i], v_buf.at[i], v_sems.at[i]) for i in range(n)]
    u_load = pltpu.make_async_copy(u_hbm.at[0, 0], u_buf, load_sems.at[1])
    for load in loads:
        load.start()

    barrier = pltpu.get_barrier_semaphore()
    for other in targets:
        pl.semaphore_signal(barrier, inc=1, device_id={"tile": other}, device_id_type=MESH)
    for hop in range(1, nf):
        pl.semaphore_signal(
            barrier, inc=1, device_id={"freq": (freq + hop) % nf}, device_id_type=MESH
        )

    for load in v_loads:
        load.start()

    def receiver_of(q):
        group = (freq // gs + 1 + q // gs) % ng
        return group * gs + (q % gs if q < nf - gs else (freq + 1 + q) % gs)

    def send(p, k):
        q, count = pieces[p]
        return pltpu.make_async_remote_copy(
            src_ref=sending.at[k, pl.ds(receiver_of(q), count)],
            dst_ref=landing.at[tile, pl.ds(q, count)],
            send_sem=send_sems.at[p, k],
            recv_sem=recv_sems.at[p, tile],
            device_id={"tile": targets[k]},
            device_id_type=MESH,
        )

    def arrival(p, k):
        q, count = pieces[p]
        return pltpu.make_async_remote_copy(
            src_ref=sending.at[k, pl.ds(receiver_of(q), count)],
            dst_ref=landing.at[targets[k], pl.ds(q, count)],
            send_sem=send_sems.at[p, k],
            recv_sem=recv_sems.at[p, targets[k]],
            device_id={"tile": targets[k]},
            device_id_type=MESH,
        )

    def spec_send(q):
        return pltpu.make_async_remote_copy(
            src_ref=spec_sending.at[q],
            dst_ref=spec_landing.at[freq],
            send_sem=spec_send_sems.at[q],
            recv_sem=spec_recv_sems.at[freq],
            device_id={"freq": receiver_of(q)},
            device_id_type=MESH,
        )

    def spec_arrival(q, source):
        return pltpu.make_async_remote_copy(
            src_ref=spec_sending.at[q],
            dst_ref=spec_landing.at[source],
            send_sem=spec_send_sems.at[q],
            recv_sem=spec_recv_sems.at[source],
            device_id={"freq": receiver_of(q)},
            device_id_type=MESH,
        )

    for load in loads:
        load.wait()
    x_t = x_buf[...].T
    for load in v_loads:
        load.wait()
    u_load.start()

    lane = lax.broadcasted_iota(jnp.int32, (sources, width), 1)

    def make_block(k, slot):
        row = order[slot]
        rank = ranks[row, tile]
        product = jnp.dot(x_t, v_buf[row], preferred_element_type=jnp.float32)
        keep = lane < rank
        real = product[:sources, :width] + product[sources:, width:]
        imag = product[sources:, :width] - product[:sources, width:]
        real = jnp.where(keep, real, 0.0).astype(jnp.bfloat16)
        imag = jnp.where(keep, imag, 0.0).astype(jnp.bfloat16)
        for c in range(nf):
            sending[k, c, 0] = real[c * chunk:(c + 1) * chunk]
            sending[k, c, 1] = imag[c * chunk:(c + 1) * chunk]

    made = set()

    def make(k):
        if k not in made:
            made.add(k)
            make_block(k, targets[k])

    for index, (p, k) in enumerate(plan):
        make(k)
        if index == 0:
            pl.semaphore_wait(barrier, n - 1 + nf - 1)
        elif index + 1 < len(plan):
            make(plan[index + 1][1])
        send(p, k).start()
    make_block(n - 1, tile)

    u_load.wait()

    def apply_rows(piece, source):
        real, imag = (piece[:, c].reshape(-1, width) for c in range(2))
        left = jnp.concatenate(
            [jnp.concatenate([real, -imag], axis=1), jnp.concatenate([imag, real], axis=1)], axis=0
        )
        return lax.dot_general(
            left, u_buf[source], (((1,), (1,)), ((), ())), preferred_element_type=jnp.float32
        )

    arrivals = near + far
    for p, (first, count) in enumerate(pieces):
        total = apply_rows(sending[n - 1, pl.ds(receiver_of(first), count)], tile)
        for k in arrivals:
            arrival(p, k).wait_recv()
            total = total + apply_rows(landing[targets[k], pl.ds(first, count)], targets[k])
        spectrum = total.astype(jnp.bfloat16).reshape(2, count, chunk, tile_rows)
        for c in range(count):
            if first + c < nf - 1:
                spec_sending[first + c] = spectrum[:, c]
                spec_send(first + c).start()
            else:
                spec_out[freq] = spectrum[:, c]

    for q in range(nf - 1):
        group = (freq // gs + ng - 1 - q // gs) % ng
        if q < nf - gs:
            sources_of = [group * gs + c for c in range(gs)] if q % gs == 0 else []
        else:
            sources_of = [group * gs + (freq + nf - 1 - q) % gs]
        for source in sources_of:
            spec_arrival(q, source).wait_recv()
            spec_out[source] = spec_landing[source]
    for p in range(len(pieces)):
        for k in range(n - 1):
            send(p, k).wait_send()
    for q in range(nf - 1):
        spec_send(q).wait_send()


def shrink_kernel(nf, nt, spec, level, out, held, sems):
    rows, tile_rows = spec.shape[2], spec.shape[3]
    half = nt // 2
    scale = 1.0 / math.sqrt(nf)
    band = 16 if rows % 16 == 0 else rows
    lanes = 128

    def coefficient(func, f, t):
        value = func(2.0 * math.pi * ((f + 1) * t % nt) / nt)
        return 0.0 if abs(value) < 1e-12 else value * scale

    lane_v = lax.broadcasted_iota(jnp.int32, (rows, rows), 1)
    row_v = lax.broadcasted_iota(jnp.int32, (rows, rows), 0)
    square = jnp.broadcast_to(level[...] * level[...], (rows, rows))
    column = jnp.sum(jnp.where(lane_v == row_v, square, 0.0), axis=1, keepdims=True)
    squares = jnp.broadcast_to(column, (rows, lanes))
    copies = []
    for r in range(0, rows, band):
        lvl = squares[r:r + band, :]
        for l in range(0, tile_rows, lanes):
            values = [
                [spec[f, c, r:r + band, l:l + lanes].astype(jnp.float32) for c in range(2)]
                for f in range(nf)
            ]
            for t in range(half):
                sums = [None, None]
                for f in range(nf):
                    kind = (f + 1) % 2
                    terms = (
                        (coefficient(math.cos, f, t), values[f][0]),
                        (-coefficient(math.sin, f, t), values[f][1]),
                    )
                    for factor, value in terms:
                        if factor == 0.0:
                            continue
                        term = value * factor
                        sums[kind] = term if sums[kind] is None else sums[kind] + term
                even, odd = sums
                for place, signal in ((t, even + odd), (t + half, even - odd)):
                    power = signal * signal
                    held[place, r:r + band, l:l + lanes] = power * signal / (power + lvl)
        copy = pltpu.make_async_copy(
            held.at[:, pl.ds(r, band)], out.at[:, pl.ds(r, band)], sems.at[r // band]
        )
        copy.start()
        copies.append(copy)
    for copy in copies:
        copy.wait()


def body(n, nf, wavefield, column_bases, row_bases, tile_ranks, row_order, shrink_level):
    _, tile_rows, double_sources = wavefield.shape
    sources = double_sources // 2
    double_width = column_bases.shape[4]
    width = double_width // 2
    chunk = sources // nf
    nt = 3 * nf
    gs = 2 if nf % 2 == 0 else 1
    ng = nf // gs
    hbm = pl.BlockSpec(memory_space=pltpu.HBM)
    vmem = pl.BlockSpec(memory_space=pltpu.VMEM)
    bf16 = jnp.bfloat16
    tables = [pltpu.with_memory_space_constraint(a, pltpu.HBM) for a in (tile_ranks, row_order)]
    spec = pl.pallas_call(
        functools.partial(exchange_kernel, n, nf, gs),
        out_shape=jax.ShapeDtypeStruct((nf, 2, chunk, tile_rows), bf16),
        in_specs=[hbm] * 5,
        out_specs=vmem,
        scratch_shapes=[
            pltpu.VMEM((tile_rows, double_sources), bf16),
            pltpu.VMEM((n, tile_rows, double_width), bf16),
            pltpu.VMEM((n, tile_rows, double_width), bf16),
            pltpu.SMEM(tile_ranks.shape, jnp.int32),
            pltpu.SMEM(row_order.shape, jnp.int32),
            pltpu.VMEM((n, nf, 2, chunk, width), bf16),
            pltpu.VMEM((n, nf, 2, chunk, width), bf16),
            pltpu.VMEM((nf - 1, 2, chunk, tile_rows), bf16),
            pltpu.VMEM((nf, 2, chunk, tile_rows), bf16),
            pltpu.SemaphoreType.DMA((4,)),
            pltpu.SemaphoreType.DMA((n,)),
            pltpu.SemaphoreType.DMA((ng - 1 + gs, n)),
            pltpu.SemaphoreType.DMA((ng - 1 + gs, n)),
            pltpu.SemaphoreType.DMA((nf,)),
            pltpu.SemaphoreType.DMA((nf,)),
        ],
        compiler_params=pltpu.CompilerParams(
            collective_id=0, has_side_effects=True, vmem_limit_bytes=56_250_000
        ),
        name="exchange",
    )(wavefield, column_bases, row_bases, *tables)
    return pl.pallas_call(
        functools.partial(shrink_kernel, nf, nt),
        out_shape=jax.ShapeDtypeStruct((nt, chunk, tile_rows), jnp.float32),
        in_specs=[vmem, vmem],
        out_specs=hbm,
        scratch_shapes=[
            pltpu.VMEM((nt, chunk, tile_rows), jnp.float32),
            pltpu.SemaphoreType.DMA((max(1, chunk // 16),)),
        ],
        compiler_params=pltpu.CompilerParams(vmem_limit_bytes=16 * 1024 * 1024),
        name="shrink",
    )(spec, shrink_level[None])


def solution(mesh):
    in_specs = (
        P("freq", "tile", None),
        P("freq", "tile", None, None, None),
        P("freq", "tile", None, None, None),
        P(),
        P(),
        P("freq"),
    )
    out_specs = P(None, "freq", "tile")
    return jax.shard_map(
        functools.partial(body, mesh.shape["tile"], mesh.shape["freq"]),
        mesh=mesh, in_specs=in_specs, out_specs=out_specs, check_vma=False,
    )
```
